32 devices in a mesh: grp: 4 (over z), row: 2 (over y), col: 4 (over x, core).
Axes of the slice: x: 2, y: 2, z: 4, core: 2. Of those that a mesh axis runs over, the one named last changes fastest.
Arguments:
- amplitudes: bfloat16 [1024, 16384], P(('grp', 'row'), 'col'), may hold values from -6 to 6
- ladder_ints: bfloat16 [16384, 16384], P('col', ('grp', 'row')), may hold values from -0.0625 to 0.0625
- tile_live: int32 [128, 128], P('col', ('grp', 'row')), may hold values 0 or 1
- cycle_direct: bfloat16 [4096, 4096], P('col', ('grp', 'row')), may hold values from -0.0625 to 0.0625
- cycle_exchange: bfloat16 [4096, 4096], P('col', ('grp', 'row')), may hold values from -0.0625 to 0.0625
- eps_occ: float32 [32], replicated, may hold values from -2 to -0.5
- eps_vir: float32 [128], replicated, may hold values from 0.5 to 3
Outputs:
- update: bfloat16 [1024, 16384], P('col', ('grp', 'row'))
The draws below stay inside these ranges and needn't reach their ends.
All inputs are finite; a program needn't handle non-finite values. No bound on the sum of `tile_live` on one device may be relied on, other than what follows from the above.
Results may differ from the reference program's by a relative error of at most 0.001.
Values may be sent and summed in bfloat16 or wider, within the bound.
A program may use at most 128 MiB of HBM per device.

```python
import jax
import jax.numpy as jnp

OCC = 32
VIR = 128
TILE = 128
OP = 1024
VP = 16384
PH = 4096


def place_ends(drawn, rng, smallest, high):
    shape = drawn.shape
    spot = [jax.random.randint(jax.random.fold_in(rng, axis), (), 0, shape[axis]) for axis in range(len(shape))]
    drawn = drawn.at[tuple(spot)].set(smallest)
    longest = shape.index(max(shape))
    spot[longest] = (spot[longest] + 1) % shape[longest]
    return drawn.at[tuple(spot)].set(high)


def block_levels(key, dims, pieces, low, high):
    def one(axis_at, blocks):
        heights = jax.random.uniform(jax.random.fold_in(jax.random.fold_in(key, 6), axis_at), (blocks,), jnp.float32, low / len(pieces), high / len(pieces))
        return jnp.repeat(jnp.exp(heights), dims[axis_at] // blocks).reshape((-1,) + (1,) * (len(dims) - axis_at - 1))

    factor_of = one(*pieces[0])
    for cut in pieces[1:]:
        factor_of = factor_of * one(*cut)
    return factor_of


def bell_draw(own_key, shape, width, bound, shards=(), held_as=jnp.bfloat16):
    drawn = width * jax.random.normal(own_key, shape, jnp.float32)
    if shards:
        drawn = drawn * block_levels(own_key, shape, shards, -0.22, 0.18)
    return jnp.clip(drawn, -bound, bound).astype(held_as)


def setup_inputs(seed: int = 0) -> dict:
    seeds = jax.random.split(jax.random.key(seed), 8)
    amplitudes = bell_draw(seeds[0], (OP, VP), 1.0, 6.0, ((0, 8), (1, 4)))
    ladder_ints = bell_draw(seeds[1], (VP, VP), (VP // 2) ** -0.5, 0.0625, ((0, 4), (1, 8)))
    tile_live = place_ends((jax.random.randint(seeds[2], (VP // TILE, VP // TILE), 0, 2) < 1).astype(jnp.int32), jax.random.fold_in(seeds[2], 1), 0, 1)
    cycle_direct = bell_draw(seeds[3], (PH, PH), (2 * PH) ** -0.5, 0.0625, ((0, 4), (1, 8)))
    cycle_exchange = bell_draw(seeds[4], (PH, PH), (2 * PH) ** -0.5, 0.0625, ((0, 4), (1, 8)))
    eps_occ = jnp.clip(jax.random.uniform(seeds[5], (OCC,), jnp.float32, -2.0, -0.5), -2.0, -0.5)
    eps_vir = jnp.clip(jax.random.uniform(seeds[6], (VIR,), jnp.float32, 0.5, 3.0), 0.5, 3.0)
    return {"amplitudes": amplitudes, "ladder_ints": ladder_ints, "tile_live": tile_live, "cycle_direct": cycle_direct, "cycle_exchange": cycle_exchange, "eps_occ": eps_occ, "eps_vir": eps_vir}


def reference(amplitudes, ladder_ints, tile_live, cycle_direct, cycle_exchange, eps_occ, eps_vir):
    expanded = jnp.repeat(jnp.repeat(tile_live, TILE, axis=0), TILE, axis=1).astype(jnp.bfloat16)
    masked = ladder_ints * expanded
    ladder = jnp.dot(amplitudes, masked, preferred_element_type=jnp.float32)
    amp_four = amplitudes.reshape(OCC, OCC, VIR, VIR)
    u_one = amp_four.transpose(0, 2, 1, 3).reshape(PH, PH)
    u_two = amp_four.transpose(0, 3, 1, 2).reshape(PH, PH)
    cycle = jnp.dot(cycle_direct, u_one, preferred_element_type=jnp.float32)
    cycle = cycle + jnp.dot(cycle_exchange, u_two, preferred_element_type=jnp.float32)
    cycle_pairs = cycle.reshape(OCC, VIR, OCC, VIR).transpose(0, 2, 1, 3).reshape(OP, VP)
    denom = (eps_vir[None, None, :, None] + eps_vir[None, None, None, :]
             - eps_occ[:, None, None, None] - eps_occ[None, :, None, None]).reshape(OP, VP)
    return ((ladder + cycle_pairs) / denom).astype(jnp.bfloat16)
```

```python
import jax
import jax.numpy as jnp
from jax import lax
from jax.sharding import PartitionSpec as P


def body(amplitudes, ladder_ints, tile_live, cycle_direct, cycle_exchange, eps_occ, eps_vir):
    groups = lax.axis_size(("grp", "row"))
    columns = lax.axis_size("col")
    col = lax.axis_index("col")
    grp = lax.axis_index(("grp", "row"))
    occ = eps_occ.shape[0]
    vir = eps_vir.shape[0]
    per_dev = occ // groups
    i_count = occ // columns
    a_count = vir // groups
    c_count = vir // columns
    f32 = jnp.float32

    x = cycle_exchange.reshape(i_count, groups, a_count, per_dev * vir)
    x = lax.all_to_all(x, ("grp", "row"), split_axis=1, concat_axis=3, tiled=True)
    x = lax.all_gather(x.reshape(i_count * a_count, occ * vir), "col", axis=0, tiled=True)

    w = cycle_direct.reshape(i_count, groups, a_count, per_dev, columns, c_count)
    w = w.transpose(1, 4, 0, 2, 3, 5).reshape(groups * columns, i_count * a_count, per_dev * c_count)
    w = lax.all_to_all(w, ("grp", "row", "col"), split_axis=0, concat_axis=0, tiled=True)
    w = w.reshape(groups, columns * i_count * a_count, per_dev * c_count)
    w = w.transpose(1, 0, 2).reshape(occ * a_count, occ * c_count)

    amps = lax.all_gather(amplitudes, ("grp", "row"), axis=0, tiled=True)
    tile_edge = ladder_ints.shape[0] // tile_live.shape[0]
    expanded = jnp.repeat(jnp.repeat(tile_live, tile_edge, axis=0), tile_edge, axis=1).astype(
        jnp.bfloat16
    )
    ladder = jnp.dot(amps, ladder_ints * expanded, preferred_element_type=f32)

    four = amps.reshape(occ, occ, c_count, vir)
    u_one = four.transpose(0, 2, 1, 3).reshape(occ * c_count, occ * vir)
    u_two = four.transpose(1, 2, 0, 3).reshape(occ * c_count, occ * vir)
    direct = jnp.dot(w, u_one, preferred_element_type=f32)
    exchange = lax.dot_general(x, u_two, (((1,), (1,)), ((), ())), preferred_element_type=f32)
    exchange = exchange.reshape(occ * a_count, occ, 1, c_count)
    exchange = jnp.broadcast_to(exchange, (occ * a_count, occ, columns, c_count)).reshape(
        occ * a_count, occ, vir
    )
    own = lax.broadcasted_iota(jnp.int32, (1, 1, vir), 2) // c_count == col
    cycle = direct.reshape(occ * a_count, occ, vir) + jnp.where(own, exchange, 0.0)
    cycle = cycle.reshape(occ, a_count, occ, vir).transpose(0, 2, 1, 3).reshape(occ * occ, a_count * vir)
    total = lax.psum_scatter(ladder + cycle, "col", scatter_dimension=0, tiled=True)

    occ_local = lax.dynamic_slice_in_dim(eps_occ, col * i_count, i_count)
    vir_local = lax.dynamic_slice_in_dim(eps_vir, grp * a_count, a_count)
    denom = (
        vir_local[None, None, :, None]
        + eps_vir[None, None, None, :]
        - occ_local[:, None, None, None]
        - eps_occ[None, :, None, None]
    ).reshape(i_count * occ, a_count * vir)
    return (total / denom).astype(jnp.bfloat16)


def solution(mesh):
    placed = (
        P(("grp", "row"), "col"),
        P("col", ("grp", "row")),
        P("col", ("grp", "row")),
        P("col", ("grp", "row")),
        P("col", ("grp", "row")),
        P(),
        P(),
    )
    return jax.shard_map(
        body, mesh=mesh, in_specs=placed, out_specs=P("col", ("grp", "row")), check_vma=False
    )
```

```python
import functools

import jax
import jax.numpy as jnp
from jax import lax
from jax.experimental import pallas as pl
from jax.experimental.pallas import tpu as pltpu
from jax.sharding import PartitionSpec as P

LIMIT = 56 * 1024 * 1024


def cycle_kernel(t_ref, w_ref, x_ref, o_ref):
    occ, step, part, vir = t_ref.shape
    col = lax.axis_index("col")
    rows = w_ref.shape[0]
    u_one = jnp.concatenate(
        [t_ref[:, j].reshape(occ * part, vir) for j in range(step)], axis=1
    )
    direct = jnp.dot(w_ref[...], u_one, preferred_element_type=jnp.float32)
    u_two = jnp.concatenate(
        [t_ref[k].reshape(step * part, vir) for k in range(occ)], axis=1
    )
    exchange = lax.dot_general(
        x_ref[...], u_two, (((1,), (1,)), ((), ())), preferred_element_type=jnp.float32
    )
    own = lax.broadcasted_iota(jnp.int32, (rows, vir), 1) // part == col
    for j in range(step):
        piece = exchange[:, j * part : (j + 1) * part]
        piece = jnp.concatenate([piece] * (vir // part), axis=1)
        o_ref[j] = direct[:, j * vir : (j + 1) * vir] + jnp.where(own, piece, 0.0)


def cycle_sum(four, w, x):
    occ, _, part, vir = four.shape
    rows = w.shape[0]
    step = 8
    return pl.pallas_call(
        cycle_kernel,
        grid=(occ // step,),
        out_shape=jax.ShapeDtypeStruct((occ, rows, vir), jnp.float32),
        in_specs=[
            pl.BlockSpec((occ, step, part, vir), lambda n: (0, n, 0, 0)),
            pl.BlockSpec(w.shape, lambda n: (0, 0)),
            pl.BlockSpec(x.shape, lambda n: (0, 0)),
        ],
        out_specs=pl.BlockSpec((step, rows, vir), lambda n: (n, 0, 0)),
        compiler_params=pltpu.CompilerParams(vmem_limit_bytes=LIMIT),
    )(four, w, x)


def ladder_kernel(live_ref, a_ref, v_ref, o_ref, held):
    edge = v_ref.shape[0] // live_ref.shape[0]
    across = v_ref.shape[1] // edge
    n = pl.program_id(0)

    @pl.when(pl.program_id(1) == 0)
    def _():
        @pl.loop(0, live_ref.shape[0])
        def _(k):
            at = pl.ds(pl.multiple_of(k * edge, edge), edge)
            for b in range(across):
                lanes = slice(b * edge, (b + 1) * edge)
                live = live_ref[k, n * across + b].astype(jnp.float32)
                held[at, lanes] = (v_ref[at, lanes].astype(jnp.float32) * live).astype(jnp.bfloat16)

    o_ref[...] = jnp.dot(a_ref[...], held[...], preferred_element_type=jnp.float32)


def ladder_sum(amps, ints, live):
    rows, depth = amps.shape
    width = ints.shape[1]
    tall = 256
    wide = min(512, width)
    return pl.pallas_call(
        ladder_kernel,
        grid=(width // wide, rows // tall),
        out_shape=jax.ShapeDtypeStruct((rows, width), jnp.float32),
        in_specs=[
            pl.BlockSpec(memory_space=pltpu.SMEM),
            pl.BlockSpec((tall, depth), lambda n, m: (m, 0)),
            pl.BlockSpec((depth, wide), lambda n, m: (0, n)),
        ],
        out_specs=pl.BlockSpec((tall, wide), lambda n, m: (m, n)),
        scratch_shapes=[pltpu.VMEM((depth, wide), jnp.bfloat16)],
        compiler_params=pltpu.CompilerParams(vmem_limit_bytes=LIMIT),
    )(live, amps, ints)


def body(amplitudes, ladder_ints, tile_live, cycle_direct, cycle_exchange, eps_occ, eps_vir):
    groups = lax.axis_size(("grp", "row"))
    columns = lax.axis_size("col")
    col = lax.axis_index("col")
    grp = lax.axis_index(("grp", "row"))
    occ = eps_occ.shape[0]
    vir = eps_vir.shape[0]
    per_dev = occ // groups
    i_count = occ // columns
    a_count = vir // groups
    c_count = vir // columns
    f32 = jnp.float32

    x = cycle_exchange.reshape(i_count, groups, a_count, per_dev * vir)
    x = lax.all_to_all(x, ("grp", "row"), split_axis=1, concat_axis=3, tiled=True)
    x = lax.all_gather(x.reshape(i_count * a_count, occ * vir), "col", axis=0, tiled=True)

    w = cycle_direct.reshape(i_count, groups, a_count, per_dev, columns, c_count)
    w = w.transpose(1, 4, 0, 2, 3, 5).reshape(groups * columns, i_count * a_count, per_dev * c_count)
    w = lax.all_to_all(w, ("grp", "row", "col"), split_axis=0, concat_axis=0, tiled=True)
    w = w.reshape(groups, columns * i_count * a_count, per_dev * c_count)
    w = w.transpose(1, 0, 2).reshape(occ * a_count, occ * c_count)

    amps = lax.all_gather(amplitudes, ("grp", "row"), axis=0, tiled=True)
    ladder = ladder_sum(amps, ladder_ints, tile_live)
    cycle = cycle_sum(amps.reshape(occ, occ, c_count, vir), w, x)
    cycle = cycle.reshape(occ, occ, a_count, vir).transpose(1, 0, 2, 3).reshape(occ * occ, a_count * vir)
    total = lax.psum_scatter(ladder + cycle, "col", scatter_dimension=0, tiled=True)

    occ_local = lax.dynamic_slice_in_dim(eps_occ, col * i_count, i_count)
    vir_local = lax.dynamic_slice_in_dim(eps_vir, grp * a_count, a_count)
    denom = (
        vir_local[None, None, :, None]
        + eps_vir[None, None, None, :]
        - occ_local[:, None, None, None]
        - eps_occ[None, :, None, None]
    ).reshape(i_count * occ, a_count * vir)
    return (total / denom).astype(jnp.bfloat16)


def solution(mesh):
    placed = (
        P(("grp", "row"), "col"),
        P("col", ("grp", "row")),
        P("col", ("grp", "row")),
        P("col", ("grp", "row")),
        P("col", ("grp", "row")),
        P(),
        P(),
    )
    return jax.shard_map(
        body, mesh=mesh, in_specs=placed, out_specs=P("col", ("grp", "row")), check_vma=False
    )
```

```python
import functools

import jax
import jax.numpy as jnp
from jax import lax
from jax.experimental import pallas as pl
from jax.experimental.pallas import tpu as pltpu
from jax.sharding import PartitionSpec as P

LIMIT = 56 * 1024 * 1024


def cycle_kernel(t_ref, w_ref, x_ref, o_ref):
    occ, step, part, vir = t_ref.shape
    col = lax.axis_index("col")
    rows = w_ref.shape[0]
    u_one = jnp.concatenate(
        [t_ref[:, j].reshape(occ * part, vir) for j in range(step)], axis=1
    )
    direct = jnp.dot(w_ref[...], u_one, preferred_element_type=jnp.float32)
    u_two = jnp.concatenate(
        [t_ref[k].reshape(step * part, vir) for k in range(occ)], axis=1
    )
    exchange = lax.dot_general(
        x_ref[...], u_two, (((1,), (1,)), ((), ())), preferred_element_type=jnp.float32
    )
    own = lax.broadcasted_iota(jnp.int32, (rows, vir), 1) // part == col
    for j in range(step):
        piece = exchange[:, j * part : (j + 1) * part]
        piece = jnp.concatenate([piece] * (vir // part), axis=1)
        o_ref[j] = direct[:, j * vir : (j + 1) * vir] + jnp.where(own, piece, 0.0)


def cycle_sum(four, w, x):
    occ, _, part, vir = four.shape
    rows = w.shape[0]
    step = 8
    return pl.pallas_call(
        cycle_kernel,
        grid=(occ // step,),
        out_shape=jax.ShapeDtypeStruct((occ, rows, vir), jnp.float32),
        in_specs=[
            pl.BlockSpec((occ, step, part, vir), lambda n: (0, n, 0, 0)),
            pl.BlockSpec(w.shape, lambda n: (0, 0)),
            pl.BlockSpec(x.shape, lambda n: (0, 0)),
        ],
        out_specs=pl.BlockSpec((step, rows, vir), lambda n: (n, 0, 0)),
        compiler_params=pltpu.CompilerParams(vmem_limit_bytes=LIMIT),
    )(four, w, x)


def ladder_kernel(live_ref, a_ref, v_ref, o_ref, held):
    edge = v_ref.shape[0] // live_ref.shape[0]
    across = v_ref.shape[1] // edge
    n = pl.program_id(0)

    @pl.when(pl.program_id(1) == 0)
    def _():
        @pl.loop(0, live_ref.shape[0])
        def _(k):
            at = pl.ds(pl.multiple_of(k * edge, edge), edge)
            for b in range(across):
                lanes = slice(b * edge, (b + 1) * edge)
                live = live_ref[k, n * across + b].astype(jnp.float32)
                held[at, lanes] = (v_ref[at, lanes].astype(jnp.float32) * live).astype(jnp.bfloat16)

    o_ref[...] = jnp.dot(a_ref[...], held[...], preferred_element_type=jnp.float32)


def ladder_sum(amps, ints, live):
    rows, depth = amps.shape
    width = ints.shape[1]
    tall = 256
    wide = min(512, width)
    return pl.pallas_call(
        ladder_kernel,
        grid=(width // wide, rows // tall),
        out_shape=jax.ShapeDtypeStruct((rows, width), jnp.float32),
        in_specs=[
            pl.BlockSpec(memory_space=pltpu.SMEM),
            pl.BlockSpec((tall, depth), lambda n, m: (m, 0)),
            pl.BlockSpec((depth, wide), lambda n, m: (0, n)),
        ],
        out_specs=pl.BlockSpec((tall, wide), lambda n, m: (m, n)),
        scratch_shapes=[pltpu.VMEM((depth, wide), jnp.bfloat16)],
        compiler_params=pltpu.CompilerParams(vmem_limit_bytes=LIMIT),
    )(live, amps, ints)


def body(amplitudes, ladder_ints, tile_live, cycle_direct, cycle_exchange, eps_occ, eps_vir):
    groups = lax.axis_size(("grp", "row"))
    columns = lax.axis_size("col")
    col = lax.axis_index("col")
    grp = lax.axis_index(("grp", "row"))
    occ = eps_occ.shape[0]
    vir = eps_vir.shape[0]
    per_dev = occ // groups
    i_count = occ // columns
    a_count = vir // groups
    c_count = vir // columns
    f32 = jnp.float32

    x = cycle_exchange.reshape(i_count, groups, a_count, per_dev * vir)
    x = lax.all_to_all(x, ("grp", "row"), split_axis=1, concat_axis=3, tiled=True)
    x = lax.all_gather(x.reshape(i_count * a_count, occ * vir), "col", axis=0, tiled=True)

    w = cycle_direct.reshape(i_count, groups, a_count, per_dev, columns, c_count)
    w = w.transpose(1, 4, 0, 2, 3, 5).reshape(groups * columns, i_count * a_count, per_dev * c_count)
    w = lax.all_to_all(w, ("grp", "row", "col"), split_axis=0, concat_axis=0, tiled=True)
    w = w.reshape(groups, columns * i_count * a_count, per_dev * c_count)
    w = w.transpose(1, 0, 2).reshape(occ * a_count, occ * c_count)

    amps = lax.all_gather(amplitudes, ("grp", "row"), axis=0, tiled=True)
    ladder = ladder_sum(amps, ladder_ints, tile_live)
    amps, ladder = lax.optimization_barrier((amps, ladder))
    cycle = cycle_sum(amps.reshape(occ, occ, c_count, vir), w, x)
    cycle = cycle.reshape(occ, occ, a_count, vir).transpose(1, 0, 2, 3).reshape(occ * occ, a_count * vir)
    total = lax.psum_scatter(ladder + cycle, "col", scatter_dimension=0, tiled=True)

    occ_local = lax.dynamic_slice_in_dim(eps_occ, col * i_count, i_count)
    vir_local = lax.dynamic_slice_in_dim(eps_vir, grp * a_count, a_count)
    denom = (
        vir_local[None, None, :, None]
        + eps_vir[None, None, None, :]
        - occ_local[:, None, None, None]
        - eps_occ[None, :, None, None]
    ).reshape(i_count * occ, a_count * vir)
    return (total / denom).astype(jnp.bfloat16)


def solution(mesh):
    placed = (
        P(("grp", "row"), "col"),
        P("col", ("grp", "row")),
        P("col", ("grp", "row")),
        P("col", ("grp", "row")),
        P("col", ("grp", "row")),
        P(),
        P(),
    )
    return jax.shard_map(
        body, mesh=mesh, in_specs=placed, out_specs=P("col", ("grp", "row")), check_vma=False
    )
```
